32 devices in a mesh: section: 2 (over y), group: 4 (over x, core), replica: 4 (over z).
Axes of the slice: x: 2, y: 2, z: 4, core: 2. Of those that a mesh axis runs over, the one named last changes fastest.
Arguments:
- block_input: bfloat16 [1, 16, 196, 512], P(None, ('group', 'replica')), may hold values from -6 to 6
- occupied: int32 [1, 16], P(None, ('group', 'replica')), may hold values 0 or 1
- cotangent: bfloat16 [1, 16, 196, 512], P(None, ('group', 'replica')), may hold values from -6 to 6
- norm1_gain: float32 [2, 512], P('section'), may hold values from 0.5 to 1.5
- norm1_bias: float32 [2, 512], P('section'), may hold values from -1.5 to 1.5
- qkv_weight: bfloat16 [2, 512, 1536], P('section', 'group'), may hold values from -0.25 to 0.25
- q_bias: float32 [2, 512], P('section'), may hold values from -2.5 to 2.5
- v_bias: float32 [2, 512], P('section'), may hold values from -2.5 to 2.5
- rel_table: float32 [2, 169, 16], P('section'), as said below
- proj_weight: bfloat16 [2, 512, 512], P('section', 'group'), may hold values from -0.75 to 0.75
- proj_bias: float32 [2, 512], P('section'), may hold values from -1.5 to 1.5
- norm2_gain: float32 [2, 512], P('section'), may hold values from 0.5 to 1.5
- norm2_bias: float32 [2, 512], P('section'), may hold values from -1.5 to 1.5
- fc1_weight: bfloat16 [2, 512, 2048], P('section', 'group'), may hold values from -0.25 to 0.25
- fc1_bias: float32 [2, 2048], P('section'), may hold values from -1.5 to 1.5
- fc2_weight: bfloat16 [2, 2048, 512], P('section', 'group'), may hold values from -0.125 to 0.125
- fc2_bias: float32 [2, 512], P('section'), may hold values from -1.5 to 1.5
Outputs:
- activations: bfloat16 [2, 1, 16, 196, 512], P('section', None, ('group', 'replica'))
- input_grads: bfloat16 [2, 1, 16, 196, 512], P('section', None, ('group', 'replica'))
- grad_norm1_gain: float32 [2, 512], P('section')
- grad_norm1_bias: float32 [2, 512], P('section')
- grad_qkv_weight: float32 [2, 512, 1536], P('section', 'group')
- grad_q_bias: float32 [2, 512], P('section')
- grad_v_bias: float32 [2, 512], P('section')
- grad_rel_table: float32 [2, 169, 16], P('section')
- grad_proj_weight: float32 [2, 512, 512], P('section', 'group')
- grad_proj_bias: float32 [2, 512], P('section')
- grad_norm2_gain: float32 [2, 512], P('section')
- grad_norm2_bias: float32 [2, 512], P('section')
- grad_fc1_weight: float32 [2, 512, 2048], P('section', 'group')
- grad_fc1_bias: float32 [2, 2048], P('section')
- grad_fc2_weight: float32 [2, 2048, 512], P('section', 'group')
- grad_fc2_bias: float32 [2, 512], P('section')
The draws below stay inside these ranges and needn't reach their ends.
Inputs may be any that keep to these rules, and one draw needn't show every extreme that they name: `rel_table`: entries of the relative-bias tables.
All inputs are finite; a program needn't handle non-finite values. No bound on the sum of `occupied` on one device may be relied on, other than what follows from the above.
Results may differ from the reference program's by a relative error of at most 0.017.
Values may be sent and summed in bfloat16 or wider, within the bound.
A program may use at most 128 MiB of HBM per device.

```python
import jax
import jax.numpy as jnp
from jax import lax

D = 512
HEADS = 16
FF = 2048
WIN = 7
SHIFT = 3
SIDE = 14
TOK_IMG = 196
TABLE = 169
LAYERS = 2
MB = 1
IMG_DEV = 1
IMAGES = 16
N_REPLICA = 4


def draw_rel_table(key, part):
    base_key = jax.random.fold_in(jax.random.fold_in(key, 17), 0)
    return jnp.clip(jax.random.normal(base_key, (LAYERS, TABLE, HEADS), jnp.float32), -4.0, 4.0)


def with_ends(values, own_key, least, high):
    longest = values.shape.index(max(values.shape))
    spots = []
    for shift in (0, 1):
        where = [jax.random.randint(jax.random.fold_in(own_key, axis), (), 0, length) for axis, length in enumerate(values.shape)]
        where[longest] = (where[longest] + shift) % values.shape[longest]
        spots.append(tuple(where))
    return values.at[spots[0]].set(least).at[spots[1]].set(high)


def level_of(stream_key, extent, cuts, smallest, largest):
    loudness = 1.0
    for axis_at, shards_of in cuts:
        steps = jax.random.uniform(jax.random.fold_in(jax.random.fold_in(stream_key, 6), axis_at), (shards_of,), jnp.float32, smallest / len(cuts), largest / len(cuts))
        loudness = loudness * jnp.repeat(jnp.exp(steps), extent[axis_at] // shards_of).reshape((-1,) + (1,) * (len(extent) - 1 - axis_at))
    return loudness


def noise(key, dims, width, limit, shards=(), held_as=jnp.bfloat16):
    drawn = jax.random.normal(key, dims, jnp.float32) * width
    if len(shards) > 0:
        drawn = level_of(key, dims, shards, -0.22, 0.18) * drawn
    return jnp.clip(drawn, min=-limit, max=limit).astype(held_as)


def setup_inputs(seed: int = 0) -> dict:
    splits = jax.random.split(jax.random.key(seed), 18)
    block_input = noise(splits[0], (MB, IMAGES, TOK_IMG, D), 1.0, 6.0, ((1, 16),))
    occupied = with_ends((jax.random.randint(splits[1], (MB, IMAGES), 0, 4) < 3).astype(jnp.int32), jax.random.fold_in(splits[1], 1), 0, 1)
    cotangent = noise(splits[2], (MB, IMAGES, TOK_IMG, D), 1.0, 6.0, ((1, 16),))
    norm1_gain = jnp.clip(1.0 + 0.1 * jax.random.normal(splits[3], (LAYERS, D), jnp.float32), 0.5, 1.5)
    norm1_bias = noise(splits[4], (LAYERS, D), 0.3, 1.5, ((0, 2),), jnp.float32)
    qkv_weight = noise(splits[5], (LAYERS, D, 3 * D), D ** -0.5, 0.25, ((0, 2), (1, 4)))
    q_bias = noise(splits[6], (LAYERS, D), 0.5, 2.5, ((0, 2),), jnp.float32)
    v_bias = noise(splits[7], (LAYERS, D), 0.5, 2.5, ((0, 2),), jnp.float32)
    rel_table = draw_rel_table(jax.random.fold_in(splits[17], 71), 0)
    proj_weight = noise(splits[9], (LAYERS, D, D), (D // 7) ** -0.5, 0.75, ((0, 2), (1, 4)))
    proj_bias = noise(splits[10], (LAYERS, D), 0.3, 1.5, ((0, 2),), jnp.float32)
    norm2_gain = jnp.clip(1.0 + 0.1 * jax.random.normal(splits[11], (LAYERS, D), jnp.float32), 0.5, 1.5)
    norm2_bias = noise(splits[12], (LAYERS, D), 0.3, 1.5, ((0, 2),), jnp.float32)
    fc1_weight = noise(splits[13], (LAYERS, D, FF), D ** -0.5, 0.25, ((0, 2), (1, 4)))
    fc1_bias = noise(splits[14], (LAYERS, FF), 0.3, 1.5, ((0, 2),), jnp.float32)
    fc2_weight = noise(splits[15], (LAYERS, FF, D), FF ** -0.5, 0.125, ((0, 2), (1, 4)))
    fc2_bias = noise(splits[16], (LAYERS, D), 0.3, 1.5, ((0, 2),), jnp.float32)
    return dict(block_input=block_input, occupied=occupied, cotangent=cotangent, norm1_gain=norm1_gain, norm1_bias=norm1_bias, qkv_weight=qkv_weight, q_bias=q_bias, v_bias=v_bias, rel_table=rel_table, proj_weight=proj_weight, proj_bias=proj_bias, norm2_gain=norm2_gain, norm2_bias=norm2_bias, fc1_weight=fc1_weight, fc1_bias=fc1_bias, fc2_weight=fc2_weight, fc2_bias=fc2_bias)


norm_eps = 1e-05
mask_fill = -100.0
root_half = 0.7071067811865476
inv_root_two_pi = 0.3989422804014327

def contract(form, former, latter):
    return jnp.einsum(form, former.astype(jnp.float32), latter.astype(jnp.float32))

def matmul(former, latter):
    return jnp.dot(former, latter, preferred_element_type=jnp.float32)

def offset_table():
    places = jnp.arange(WIN * WIN, dtype=jnp.int32)
    rowpos = places // WIN
    colpos = places % WIN
    offsets = (rowpos[:, None] - rowpos[None, :] + WIN - 1) * (2 * WIN - 1) + (colpos[:, None] - colpos[None, :] + WIN - 1)
    return (offsets.reshape(-1)[:, None] == jnp.arange(TABLE, dtype=jnp.int32)[None, :]).astype(jnp.float32)

def partition(token_grid):
    num_images = token_grid.shape[0]
    channels = token_grid.shape[3]
    across = SIDE // WIN
    shaped = token_grid.reshape(num_images, across, WIN, across, WIN, channels).transpose(0, 1, 3, 2, 4, 5)
    return shaped.reshape(num_images * across * across, WIN * WIN, channels)

def windows_back(windows, num_images):
    channels = windows.shape[-1]
    across = SIDE // WIN
    shaped = windows.reshape(num_images, across, across, WIN, WIN, channels).transpose(0, 1, 3, 2, 4, 5)
    return shaped.reshape(num_images, SIDE, SIDE, channels)

def region_mask():
    grid_cells = jnp.arange(SIDE, dtype=jnp.int32)
    band_ids = (grid_cells >= SIDE - WIN).astype(jnp.int32) + (grid_cells >= SIDE - SHIFT).astype(jnp.int32)
    labels = (band_ids[:, None] * 3 + band_ids[None, :]).astype(jnp.float32)
    windows = partition(labels[None, :, :, None])[:, :, 0]
    return jnp.where(windows[:, :, None] != windows[:, None, :], mask_fill, 0.0).astype(jnp.float32)

def roll_grid(token_grid, amount):
    return jnp.roll(jnp.roll(token_grid, amount, axis=1), amount, axis=2)

def norm_forward(values, gain_vec, bias_vec):
    centered = values - lax.optimization_barrier(jnp.mean(values, axis=-1, keepdims=True))
    scale_inv = lax.rsqrt(lax.optimization_barrier(jnp.mean(centered * centered, axis=-1, keepdims=True)) + norm_eps)
    normed = centered * scale_inv
    return (normed * gain_vec + bias_vec, normed, scale_inv)

def norm_backward(grad_normed, normed, scale_inv):
    first_mean = lax.optimization_barrier(jnp.mean(grad_normed, axis=-1, keepdims=True))
    second_mean = lax.optimization_barrier(jnp.mean(grad_normed * normed, axis=-1, keepdims=True))
    return scale_inv * (grad_normed - first_mean - normed * second_mean)

def gelu_value(pre_act):
    return 0.5 * pre_act * (1.0 + lax.erf(pre_act * root_half))

def gelu_slope(pre_act):
    return 0.5 * (1.0 + lax.erf(pre_act * root_half)) + pre_act * jnp.exp(-0.5 * pre_act * pre_act) * inv_root_two_pi

def score_block(query_rows, key_rows, table, onehot, masks, mask_scale, num_images):
    num_heads = table.shape[1]
    win_area = WIN * WIN
    rel_bias = jnp.dot(onehot, table, precision=lax.Precision.HIGHEST).T.reshape(num_heads, win_area, win_area)
    scores = contract('wqhd,wkhd->whqk', query_rows, key_rows) + rel_bias[None]
    per_image = masks.shape[0]
    scores = scores.reshape(num_images, per_image, num_heads, win_area, win_area) + mask_scale * masks[None, :, None]
    return scores.reshape(num_images * per_image, num_heads, win_area, win_area)

def layer_forward(layer_in, live_rows, params, amount, mask_scale, onehot, masks):
    gain_one, bias_one, w_qkv, query_bias, value_bias, table, w_proj, proj_shift, gain_two, bias_two, w_up, up_shift, w_down, down_shift = params
    num_images = layer_in.shape[0]
    model_width = layer_in.shape[2]
    num_heads = table.shape[1]
    head_dim = model_width // num_heads
    shaped = (-1, WIN * WIN, num_heads, head_dim)
    values = layer_in.astype(jnp.float32)
    normed_one, unit_one, inv_one = norm_forward(values, gain_one, bias_one)
    token_grid = roll_grid(normed_one.astype(jnp.bfloat16).reshape(num_images, SIDE, SIDE, model_width), -amount)
    windows = partition(token_grid).reshape(-1, model_width)
    qkv_rows = matmul(windows, w_qkv)
    query_rows = ((qkv_rows[:, :model_width] + query_bias) * head_dim ** (-0.5)).astype(jnp.bfloat16)
    key_rows = qkv_rows[:, model_width:2 * model_width].astype(jnp.bfloat16)
    value_rows = (qkv_rows[:, 2 * model_width:] + value_bias).astype(jnp.bfloat16)
    scores = score_block(query_rows.reshape(shaped), key_rows.reshape(shaped), table, onehot, masks, mask_scale, num_images)
    row_peak = lax.optimization_barrier(jnp.max(scores, axis=-1, keepdims=True))
    exp_scores = jnp.exp(scores - row_peak)
    row_total = lax.optimization_barrier(jnp.sum(exp_scores, axis=-1, keepdims=True))
    log_total = row_peak + jnp.log(row_total)
    attn_probs = (exp_scores / row_total).astype(jnp.bfloat16)
    attended = contract('whqk,wkhd->wqhd', attn_probs, value_rows.reshape(shaped)).astype(jnp.bfloat16).reshape(-1, model_width)
    projected = matmul(attended, w_proj) + proj_shift
    branch = roll_grid(windows_back(projected.reshape(-1, WIN * WIN, model_width), num_images), amount)
    residual = values + branch.reshape(num_images, SIDE * SIDE, model_width)
    normed_two, unit_two, inv_two = norm_forward(residual, gain_two, bias_two)
    normed_low = normed_two.astype(jnp.bfloat16).reshape(-1, model_width)
    pre_act = matmul(normed_low, w_up) + up_shift
    hidden = gelu_value(pre_act).astype(jnp.bfloat16)
    result = residual + (matmul(hidden, w_down) + down_shift).reshape(residual.shape)
    layer_out = (result * live_rows[:, None, None]).astype(jnp.bfloat16)
    saved_state = (unit_one, inv_one, windows, query_rows, key_rows, value_rows, log_total, attended, unit_two, inv_two, normed_low, pre_act, hidden)
    return (layer_out, saved_state)

def layer_backward(saved_state, grad_out, live_rows, params, amount, mask_scale, onehot, masks):
    gain_one, bias_one, w_qkv, query_bias, value_bias, table, w_proj, proj_shift, gain_two, bias_two, w_up, up_shift, w_down, down_shift = params
    unit_one, inv_one, windows, query_rows, key_rows, value_rows, log_total, attended, unit_two, inv_two, normed_low, pre_act, hidden = saved_state
    num_images = grad_out.shape[0]
    model_width = grad_out.shape[2]
    num_heads = table.shape[1]
    head_dim = model_width // num_heads
    shaped = (-1, WIN * WIN, num_heads, head_dim)
    image_shape = (num_images, SIDE * SIDE, model_width)
    upstream = (grad_out.astype(jnp.float32) * live_rows[:, None, None]).reshape(-1, model_width)
    upstream_low = upstream.astype(jnp.bfloat16)
    grad_down = matmul(hidden.T, upstream_low)
    grad_down_bias = lax.optimization_barrier(jnp.sum(upstream, axis=0))
    grad_pre = matmul(upstream_low, w_down.T) * gelu_slope(pre_act)
    grad_pre_low = grad_pre.astype(jnp.bfloat16)
    grad_up = matmul(normed_low.T, grad_pre_low)
    grad_up_bias = lax.optimization_barrier(jnp.sum(grad_pre, axis=0))
    grad_normed_two = matmul(grad_pre_low, w_up.T).reshape(image_shape)
    grad_gain_two = lax.optimization_barrier(jnp.sum(grad_normed_two * unit_two, axis=(0, 1)))
    grad_bias_two = lax.optimization_barrier(jnp.sum(grad_normed_two, axis=(0, 1)))
    grad_resid = upstream.reshape(image_shape) + norm_backward(grad_normed_two * gain_two, unit_two, inv_two)
    grad_proj_bias = lax.optimization_barrier(jnp.sum(grad_resid, axis=(0, 1)))
    grad_branch = partition(roll_grid(grad_resid.reshape(num_images, SIDE, SIDE, model_width), -amount))
    grad_branch = grad_branch.reshape(-1, model_width).astype(jnp.bfloat16)
    grad_proj = matmul(attended.T, grad_branch)
    grad_attended = matmul(grad_branch, w_proj.T).astype(jnp.bfloat16).reshape(shaped)
    scores = score_block(query_rows.reshape(shaped), key_rows.reshape(shaped), table, onehot, masks, mask_scale, num_images)
    attn_probs = jnp.exp(scores - log_total)
    probs_low = attn_probs.astype(jnp.bfloat16)
    grad_values = contract('whqk,wqhd->wkhd', probs_low, grad_attended).reshape(-1, model_width)
    grad_probs = contract('wqhd,wkhd->whqk', grad_attended, value_rows.reshape(shaped))
    row_delta = lax.optimization_barrier(jnp.sum(attn_probs * grad_probs, axis=-1, keepdims=True))
    grad_scores = attn_probs * (grad_probs - row_delta)
    grad_table = jnp.dot(lax.optimization_barrier(jnp.sum(grad_scores, axis=0)).reshape(num_heads, -1), onehot, precision=lax.Precision.HIGHEST).T
    scores_low = grad_scores.astype(jnp.bfloat16)
    grad_query = contract('whqk,wkhd->wqhd', scores_low, key_rows.reshape(shaped)).reshape(-1, model_width) * head_dim ** (-0.5)
    grad_keys = contract('whqk,wqhd->wkhd', scores_low, query_rows.reshape(shaped)).reshape(-1, model_width)
    grad_q_bias = lax.optimization_barrier(jnp.sum(grad_query, axis=0))
    grad_v_bias = lax.optimization_barrier(jnp.sum(grad_values, axis=0))
    grad_qkv_low = jnp.concatenate([grad_query, grad_keys, grad_values], axis=1).astype(jnp.bfloat16)
    grad_qkv = matmul(windows.T, grad_qkv_low)
    grad_normed_one = matmul(grad_qkv_low, w_qkv.T).reshape(-1, WIN * WIN, model_width)
    grad_normed_one = roll_grid(windows_back(grad_normed_one, num_images), amount).reshape(image_shape)
    grad_gain_one = lax.optimization_barrier(jnp.sum(grad_normed_one * unit_one, axis=(0, 1)))
    grad_bias_one = lax.optimization_barrier(jnp.sum(grad_normed_one, axis=(0, 1)))
    grad_in = (grad_resid + norm_backward(grad_normed_one * gain_one, unit_one, inv_one)).astype(jnp.bfloat16)
    return (grad_in, (grad_gain_one, grad_bias_one, grad_qkv, grad_q_bias, grad_v_bias, grad_table, grad_proj, grad_proj_bias, grad_gain_two, grad_bias_two, grad_up, grad_up_bias, grad_down, grad_down_bias))

def reference(block_input, occupied, cotangent, norm1_gain, norm1_bias, qkv_weight, q_bias, v_bias, rel_table, proj_weight, proj_bias, norm2_gain, norm2_bias, fc1_weight, fc1_bias, fc2_weight, fc2_bias):
    onehot = offset_table()
    masks = region_mask()
    stacked = (norm1_gain, norm1_bias, qkv_weight, q_bias, v_bias, rel_table, proj_weight, proj_bias, norm2_gain, norm2_bias, fc1_weight, fc1_bias, fc2_weight, fc2_bias)
    first_params = tuple((weight_arg[0] for weight_arg in stacked))
    second_params = tuple((weight_arg[1] for weight_arg in stacked))
    block_images = IMG_DEV * N_REPLICA
    num_blocks = IMAGES // block_images

    def one_block(carry, pieces):
        inputs_block, occupied_block, cot_block = pieces
        live_rows = occupied_block.astype(jnp.float32)
        first_out, first_saved = layer_forward(inputs_block, live_rows, first_params, 0, 0.0, onehot, masks)
        second_out, second_saved = layer_forward(first_out, live_rows, second_params, SHIFT, 1.0, onehot, masks)
        second_grad, second_terms = layer_backward(second_saved, cot_block, live_rows, second_params, SHIFT, 1.0, onehot, masks)
        first_grad, first_terms = layer_backward(first_saved, second_grad, live_rows, first_params, 0, 0.0, onehot, masks)
        carry = jax.tree.map(lambda total, term: total + term, carry, (first_terms, second_terms))
        return (carry, (first_out, second_out, first_grad, second_grad))
    carry = jax.tree.map(lambda leaf: jnp.zeros(leaf.shape, jnp.float32), (first_params, second_params))
    first_outs, second_outs, first_grads, second_grads = ([], [], [], [])
    block_shape = (num_blocks, block_images, TOK_IMG, D)
    for micro in range(MB):
        pieces = (block_input[micro].reshape(block_shape), occupied[micro].reshape(num_blocks, block_images), cotangent[micro].reshape(block_shape))
        carry, results = lax.scan(one_block, carry, pieces)
        first_outs.append(results[0].reshape(IMAGES, TOK_IMG, D))
        second_outs.append(results[1].reshape(IMAGES, TOK_IMG, D))
        first_grads.append(results[2].reshape(IMAGES, TOK_IMG, D))
        second_grads.append(results[3].reshape(IMAGES, TOK_IMG, D))
    activations = jnp.stack([jnp.stack(first_outs), jnp.stack(second_outs)])
    input_grads = jnp.stack([jnp.stack(first_grads), jnp.stack(second_grads)])
    grads = [jnp.stack([carry[0][position], carry[1][position]]) for position in range(14)]
    return (activations, input_grads, grads[0], grads[1], grads[2], grads[3], grads[4], grads[5], grads[6], grads[7], grads[8], grads[9], grads[10], grads[11], grads[12], grads[13])
```

```python
import functools

import jax
import jax.numpy as jnp
from jax import lax
from jax.experimental import pallas as pl
from jax.experimental.pallas import tpu as pltpu
from jax.sharding import PartitionSpec as P

WIN = 7
SHIFT = 3
SIDE = 14
TABLE = 169


norm_eps = 1e-05
mask_fill = -100.0
root_half = 0.7071067811865476
inv_root_two_pi = 0.3989422804014327

MESH = pl.DeviceIdType.MESH


def rounds_of(devices):
    count = devices.bit_length() - 1
    assert devices == 1 << count, "power"
    return count


def chain_place(rank, devices):
    half = devices // 2
    left = rank < half
    is_mid = (rank == half - 1) | (rank == half)
    has_outer = (left & (rank > 0)) | (~left & (rank < devices - 1))
    inner = jnp.where(left, rank + 1, rank - 1)
    outer = jnp.where(left, jnp.maximum(rank - 1, 0), jnp.minimum(rank + 1, devices - 1))
    return is_mid, has_outer, inner, outer


def greet(partners, wait_extra):
    barrier = pltpu.get_barrier_semaphore()
    for device in partners:
        pl.semaphore_signal(barrier, inc=1, device_id=device, device_id_type=MESH)
    pl.semaphore_wait(barrier, len(partners) + wait_extra)


def reduce_kernel(
    groups,
    replicas,
    grads,
    small,
    total_out,
    small_out,
    *scratch,
):
    rounds = rounds_of(groups)
    recv_bufs = scratch[:rounds]
    acc_bufs = scratch[rounds : 2 * rounds]
    (
        chain_buf,
        total_buf,
        small_send,
        small_recv,
        send_sem,
        recv_sem,
        chain_send,
        chain_recv,
        back_send,
        back_recv,
        small_ssem,
        small_rsem,
    ) = scratch[2 * rounds :]
    chunks = grads.shape[0]
    me = lax.axis_index("group")
    rank = lax.axis_index("replica")
    is_mid, has_outer, inner, outer = chain_place(rank, replicas)
    bits = [lax.rem(me // (1 << r), 2) for r in range(rounds)]
    partners = [me + (1 - 2 * bits[r]) * (1 << r) for r in range(rounds)]

    barrier = pltpu.get_barrier_semaphore()
    for partner in partners:
        pl.semaphore_signal(barrier, inc=1, device_id={"group": partner}, device_id_type=MESH)
    pl.semaphore_signal(barrier, inc=1, device_id={"replica": inner}, device_id_type=MESH)

    @pl.when(has_outer)
    def _():
        pl.semaphore_signal(barrier, inc=1, device_id={"replica": outer}, device_id_type=MESH)

    pl.semaphore_wait(barrier, rounds + 1 + has_outer.astype(jnp.int32))

    def round_copy(r, j, u):
        source = grads if r == 0 else acc_bufs[r - 1]
        return pltpu.make_async_remote_copy(
            src_ref=source.at[j, 2 * u + 1 - bits[r]],
            dst_ref=recv_bufs[r].at[j, u],
            send_sem=send_sem.at[r, j, u],
            recv_sem=recv_sem.at[r, j, u],
            device_id={"group": partners[r]},
            device_id_type=MESH,
        )

    mid_slot = is_mid.astype(jnp.int32)

    def chain_copy(j, slot):
        return pltpu.make_async_remote_copy(
            src_ref=acc_bufs[rounds - 1].at[j, 0],
            dst_ref=chain_buf.at[slot, j],
            send_sem=chain_send.at[j],
            recv_sem=chain_recv.at[slot, j],
            device_id={"replica": inner},
            device_id_type=MESH,
        )

    def back_copy(j):
        return pltpu.make_async_remote_copy(
            src_ref=total_buf.at[j],
            dst_ref=total_buf.at[j],
            send_sem=back_send.at[j],
            recv_sem=back_recv.at[j],
            device_id={"replica": outer},
            device_id_type=MESH,
        )

    def small_copy(k, slot, target):
        return pltpu.make_async_remote_copy(
            src_ref=small_send.at[k],
            dst_ref=small_recv.at[slot],
            send_sem=small_ssem.at[k],
            recv_sem=small_rsem.at[slot],
            device_id=target,
            device_id_type=MESH,
        )

    def add_up(former, latter):
        return (former.astype(jnp.float32) + latter.astype(jnp.float32)).astype(jnp.bfloat16)

    def fold_round(r, j):
        for u in range(groups >> (r + 1)):
            round_copy(r, j, u).wait_recv()
            source = grads if r == 0 else acc_bufs[r - 1]
            acc_bufs[r][j, u] = add_up(source[j, 2 * u + bits[r]], recv_bufs[r][j, u])
        if r + 1 < rounds:
            for u in range(groups >> (r + 2)):
                round_copy(r + 1, j, u).start()
        else:

            @pl.when(~has_outer)
            def _():
                chain_copy(j, mid_slot).start()

    last = acc_bufs[rounds - 1]

    def from_outer(j):
        @pl.when(has_outer)
        def _():
            chain_copy(j, 0).wait_recv()
            last[j, 0] = add_up(last[j, 0], chain_buf[0, j])
            chain_copy(j, mid_slot).start()

    def meet(j):
        @pl.when(is_mid)
        def _():
            chain_copy(j, 1).wait_recv()
            total_buf[j] = add_up(last[j, 0], chain_buf[1, j])

        @pl.when(~is_mid)
        def _():
            back_copy(j).wait_recv()

        @pl.when(has_outer)
        def _():
            back_copy(j).start()

        total_out[j] = total_buf[j].astype(jnp.float32)

    small_send[0] = small[...]
    if rounds > 0:
        small_copy(0, 0, {"group": partners[0]}).start()

    @pl.loop(0, chunks)
    def _(j):
        for u in range(groups // 2):
            round_copy(0, j, u).start()

    def small_step(k):
        if k < rounds:
            small_copy(k, k, {"group": partners[k]}).wait_recv()
            small_send[k + 1] = small_send[k] + small_recv[k]
            if k + 1 < rounds:
                small_copy(k + 1, k + 1, {"group": partners[k + 1]}).start()
            else:

                @pl.when(~has_outer)
                def _():
                    small_copy(rounds, rounds + mid_slot, {"replica": inner}).start()
        elif k == rounds:

            @pl.when(has_outer)
            def _():
                small_copy(rounds, rounds, {"replica": inner}).wait_recv()
                small_send[rounds] = small_send[rounds] + small_recv[rounds]
                small_copy(rounds, rounds + mid_slot, {"replica": inner}).start()
        else:

            @pl.when(is_mid)
            def _():
                small_copy(rounds, rounds + 1, {"replica": inner}).wait_recv()
                small_send[rounds + 1] = small_send[rounds] + small_recv[rounds + 1]

            @pl.when(~is_mid)
            def _():
                small_copy(rounds + 1, rounds + 2, {"replica": outer}).wait_recv()
                small_send[rounds + 1] = small_recv[rounds + 2]

            @pl.when(has_outer)
            def _():
                small_copy(rounds + 1, rounds + 2, {"replica": outer}).start()

            small_out[...] = small_send[rounds + 1]

    stages = [functools.partial(fold_round, r) for r in range(rounds)] + [from_outer, meet]

    @pl.loop(0, chunks + len(stages) - 1)
    def _(step):
        for depth, stage in enumerate(stages):
            j = step - depth

            @pl.when((j >= 0) & (j < chunks))
            def _():
                stage(j)

            @pl.when(step == depth)
            def _():
                small_step(depth)

    @pl.loop(0, chunks)
    def _(j):
        for r in range(rounds):
            for u in range(groups >> (r + 1)):
                round_copy(r, j, u).wait_send()
        chain_copy(j, mid_slot).wait_send()

        @pl.when(has_outer)
        def _():
            back_copy(j).wait_send()

    for k in range(rounds):
        small_copy(k, k, {"group": partners[k]}).wait_send()
    small_copy(rounds, rounds + mid_slot, {"replica": inner}).wait_send()

    @pl.when(has_outer)
    def _():
        small_copy(rounds + 1, rounds + 2, {"replica": outer}).wait_send()


def reduce_all(grads, small, groups, replicas):
    chunks, _, rows, cols = grads.shape
    rounds = rounds_of(groups)
    low = jnp.bfloat16
    halves = [groups >> (r + 1) for r in range(rounds)]
    scratch = (
        [pltpu.VMEM((chunks, half, rows, cols), low) for half in halves]
        + [pltpu.VMEM((chunks, half, rows, cols), low) for half in halves]
        + [
            pltpu.VMEM((2, chunks, rows, cols), low),
            pltpu.VMEM((chunks, rows, cols), low),
            pltpu.VMEM((rounds + 2,) + small.shape, jnp.float32),
            pltpu.VMEM((rounds + 3,) + small.shape, jnp.float32),
            pltpu.SemaphoreType.DMA((rounds, chunks, groups // 2)),
            pltpu.SemaphoreType.DMA((rounds, chunks, groups // 2)),
            pltpu.SemaphoreType.DMA((chunks,)),
            pltpu.SemaphoreType.DMA((2, chunks)),
            pltpu.SemaphoreType.DMA((chunks,)),
            pltpu.SemaphoreType.DMA((chunks,)),
            pltpu.SemaphoreType.DMA((rounds + 2,)),
            pltpu.SemaphoreType.DMA((rounds + 3,)),
        ]
    )
    return pl.pallas_call(
        functools.partial(reduce_kernel, groups, replicas),
        out_shape=(
            jax.ShapeDtypeStruct((chunks, rows, cols), jnp.float32),
            jax.ShapeDtypeStruct(small.shape, jnp.float32),
        ),
        in_specs=[pl.BlockSpec(memory_space=pltpu.VMEM)] * 2,
        out_specs=[pl.BlockSpec(memory_space=pltpu.VMEM)] * 2,
        scratch_shapes=scratch,
        compiler_params=pltpu.CompilerParams(
            collective_id=1, has_side_effects=True, vmem_limit_bytes=60 * 1024 * 1024
        ),
        name="grad_reduce",
    )(grads, small)


def gather_kernel(groups, *refs):
    count = len(refs) // 2 - 1
    parts = refs[:count]
    wholes = refs[count : 2 * count]
    own_sem, send_sem, recv_sem = refs[2 * count :]
    rounds = rounds_of(groups)
    me = lax.axis_index("group")
    order = [r for r in range(1, rounds)] + [0]
    bits = [lax.rem(me // (1 << r), 2) for r in range(rounds)]
    partners = [me + (1 - 2 * bits[r]) * (1 << r) for r in range(rounds)]
    greet([{"group": partner} for partner in partners], 0)

    def rows_of(i, device):
        height = parts[i].shape[0]
        return wholes[i].at[pl.ds(pl.multiple_of(device * height, height), height), :]

    def held(step):
        devices = [me]
        for r in order[:step]:
            devices = devices + [d + (1 - 2 * bits[r]) * (1 << r) for d in devices]
        return devices

    def piece(i, step, k):
        device = held(step)[k]
        source = parts[i] if k == 0 else rows_of(i, device)
        return pltpu.make_async_remote_copy(
            src_ref=source,
            dst_ref=rows_of(i, device),
            send_sem=send_sem.at[i, step, k],
            recv_sem=recv_sem.at[i, step, k],
            device_id={"group": partners[order[step]]},
            device_id_type=MESH,
        )

    for i in range(count):
        for step in range(rounds):
            piece(i, step, 0).start()
    own = [pltpu.make_async_copy(parts[i], rows_of(i, me), own_sem.at[i]) for i in range(count)]
    for copy in own:
        copy.start()
    for i in range(count):
        for step in range(rounds):
            for k in range(1 << step):
                piece(i, step, k).wait_recv()
                index = k + (1 << step)
                for later in range(step + 1, rounds):
                    piece(i, later, index).start()
    for copy in own:
        copy.wait()
    for i in range(count):
        for step in range(rounds):
            for k in range(1 << step):
                piece(i, step, k).wait_send()


def gather_all(parts, groups):
    count = len(parts)
    rounds = rounds_of(groups)
    return pl.pallas_call(
        functools.partial(gather_kernel, groups),
        out_shape=[
            jax.ShapeDtypeStruct((groups * part.shape[0], part.shape[1]), part.dtype)
            for part in parts
        ],
        in_specs=[pl.BlockSpec(memory_space=pltpu.VMEM)] * count,
        out_specs=[pl.BlockSpec(memory_space=pltpu.VMEM)] * count,
        scratch_shapes=[
            pltpu.SemaphoreType.DMA((count,)),
            pltpu.SemaphoreType.DMA((count, rounds, groups // 2)),
            pltpu.SemaphoreType.DMA((count, rounds, groups // 2)),
        ],
        compiler_params=pltpu.CompilerParams(collective_id=2, has_side_effects=True),
        name="weight_gather",
    )(*parts)


def pack_small(terms, width):
    flat = jnp.concatenate([term.reshape(-1) for term in terms])
    rows = -(-flat.shape[0] // width)
    rows = -(-rows // 8) * 8
    return jnp.pad(flat, (0, rows * width - flat.shape[0])).reshape(rows, width)


def unpack_small(packed, terms):
    flat = packed.reshape(-1)
    found = []
    start = 0
    for term in terms:
        found.append(flat[start : start + term.size].reshape(term.shape))
        start += term.size
    return found


def passed_along(shard, axis, by):
    devices = lax.axis_size(axis)
    pairs = [(i, i + by) for i in range(devices) if 0 <= i + by < devices]
    return lax.ppermute(shard, axis, pairs)


def norm_forward(values, gain_vec, bias_vec):
    centered = values - jnp.mean(values, axis=-1, keepdims=True)
    scale_inv = lax.rsqrt(jnp.mean(centered * centered, axis=-1, keepdims=True) + norm_eps)
    normed = centered * scale_inv
    return (normed * gain_vec + bias_vec, normed, scale_inv)


def norm_backward(grad_normed, normed, scale_inv):
    first_mean = jnp.mean(grad_normed, axis=-1, keepdims=True)
    second_mean = jnp.mean(grad_normed * normed, axis=-1, keepdims=True)
    return scale_inv * (grad_normed - first_mean - normed * second_mean)


def gelu_value(pre_act):
    return 0.5 * pre_act * (1.0 + lax.erf(pre_act * root_half))


def gelu_slope(pre_act):
    return (
        0.5 * (1.0 + lax.erf(pre_act * root_half))
        + pre_act * jnp.exp(-0.5 * pre_act * pre_act) * inv_root_two_pi
    )


NEG = -1e30
LOW = jnp.bfloat16
PADDED = 64


def up_to(count, step):
    return -(-count // step) * step


def div_win(values):
    return jnp.right_shift(values * 37, 8)


def dot_rows(former, latter):
    return lax.dot_general(former, latter, (((1,), (0,)), ((), ())), preferred_element_type=jnp.float32)


def dot_last(former, latter):
    return lax.dot_general(former, latter, (((1,), (1,)), ((), ())), preferred_element_type=jnp.float32)


def dot_first(former, latter):
    return lax.dot_general(former, latter, (((0,), (0,)), ((), ())), preferred_element_type=jnp.float32)


def place_of(slot, amount):
    window = jnp.right_shift(slot, 6)
    inside = jnp.bitwise_and(slot, PADDED - 1)
    in_row = div_win(inside)
    row = jnp.right_shift(window, 1) * WIN + in_row
    col = jnp.bitwise_and(window, 1) * WIN + inside - in_row * WIN
    held = inside < WIN * WIN
    old_row = row + amount
    old_row = jnp.where(old_row >= SIDE, old_row - SIDE, old_row)
    old_col = col + amount
    old_col = jnp.where(old_col >= SIDE, old_col - SIDE, old_col)
    token = jnp.where(held, old_row * SIDE + old_col, -1)
    return window, row, col, token, held


def movers(tokens, amount):
    slots = (SIDE // WIN) ** 2 * PADDED
    down = lax.broadcasted_iota(jnp.int32, (slots, tokens), 0)
    across = lax.broadcasted_iota(jnp.int32, (slots, tokens), 1)
    to_windows = (place_of(down, amount)[3] == across).astype(jnp.float32).astype(LOW)
    down = lax.broadcasted_iota(jnp.int32, (tokens, slots), 0)
    across = lax.broadcasted_iota(jnp.int32, (tokens, slots), 1)
    to_grid = (place_of(across, amount)[3] == down).astype(jnp.float32).astype(LOW)
    return to_windows, to_grid


def move(mover, values):
    return dot_rows(mover, values).astype(LOW)


def pair_mask(pair, amount, factor):
    def parts(axis):
        slot = lax.broadcasted_iota(jnp.int32, (2 * PADDED, 2 * PADDED), axis) + pair * 2 * PADDED
        window, row, col, _, held = place_of(slot, amount)
        bands = []
        for line in (row, col):
            bands.append(
                (line >= SIDE - WIN).astype(jnp.int32) + (line >= SIDE - SHIFT).astype(jnp.int32)
            )
        return window, 3 * bands[0] + bands[1], held

    window_q, label_q, _ = parts(0)
    window_k, label_k, held_k = parts(1)
    mask = jnp.where(label_q != label_k, mask_fill * factor, 0.0)
    return jnp.where((window_q == window_k) & held_k, mask, NEG)


def head_lanes(head_dim, dtype):
    lane = lax.broadcasted_iota(jnp.int32, (2 * PADDED, 128), 1)
    return [
        ((lane >= h * head_dim) & (lane < (h + 1) * head_dim)).astype(jnp.float32).astype(dtype)
        for h in range(128 // head_dim)
    ]


def forward_kernel(
    x_ref, live_ref, gain1, bias1, wqkv, qb, vb, bias_ref, wproj, projb, gain2, bias2, wup, upb, wdown, downb,
    act_ref, q_ref, k_ref, v_ref, p_ref, att_ref, resid_ref, pre_ref, n1_ref, n2_ref, hid_ref, x32,
):
    section = lax.axis_index("section")
    amount = SHIFT * section
    factor = section.astype(jnp.float32)
    count, width = x_ref.shape
    tokens = x32.shape[0]
    heads = bias_ref.shape[0]
    head_dim = width // heads
    x32[...] = jnp.zeros_like(x32)
    x32[:count, :] = x_ref[...].astype(jnp.float32)
    to_windows, to_grid = movers(tokens, amount)
    normed, _, _ = norm_forward(x32[...], gain1[...], bias1[...])
    n1_ref[...] = normed.astype(LOW)
    query = dot_rows(n1_ref[...], wqkv[:, :width]) + qb[...]
    q_ref[...] = move(to_windows, (query * head_dim ** (-0.5)).astype(LOW))
    k_ref[...] = move(to_windows, dot_rows(n1_ref[...], wqkv[:, width : 2 * width]).astype(LOW))
    v_ref[...] = move(to_windows, (dot_rows(n1_ref[...], wqkv[:, 2 * width :]) + vb[...]).astype(LOW))
    lanes = head_lanes(head_dim, LOW)
    per = len(lanes)
    columns = []
    for pair in range(2):
        mask = pair_mask(pair, amount, factor)
        rows = slice(pair * 2 * PADDED, (pair + 1) * 2 * PADDED)
        found = []
        for block in range(width // 128):
            cols = slice(block * 128, (block + 1) * 128)
            q, k, v = q_ref[rows, cols], k_ref[rows, cols], v_ref[rows, cols]
            probs = []
            values = []
            for h in range(per):
                scores = dot_last(q * lanes[h], k) + bias_ref[block * per + h] + mask
                raised = jnp.exp(scores - jnp.max(scores, axis=-1, keepdims=True))
                full = raised / jnp.sum(raised, axis=-1, keepdims=True)
                p_ref[pair * heads + block * per + h] = full
                probs.append(full.astype(LOW))
                values.append(v * lanes[h])
            found.append(
                dot_rows(jnp.concatenate(probs, axis=1), jnp.concatenate(values, axis=0)).astype(LOW)
            )
        columns.append(jnp.concatenate(found, axis=1))
    attended = move(to_grid, jnp.concatenate(columns, axis=0))
    att_ref[...] = attended
    resid = x32[...] + (dot_rows(attended, wproj[...]) + projb[...])
    resid_ref[...] = resid
    normed, _, _ = norm_forward(resid, gain2[...], bias2[...])
    n2_ref[...] = normed.astype(LOW)
    for start in range(0, wup.shape[1], width):
        cols = slice(start, start + width)
        pre = dot_rows(n2_ref[...], wup[:, cols]) + upb[:, cols]
        pre_ref[:, cols] = pre
        hid_ref[:, cols] = gelu_value(pre).astype(LOW)
    result = resid_ref[...] + (dot_rows(hid_ref[...], wdown[...]) + downb[...])
    act_ref[...] = (result * live_ref[0, 0])[:count].astype(LOW)


def backward_kernel(
    x_ref, grad_ref, live_ref, gain1, wqkv, wproj, gain2, wup, wdown,
    q_ref, k_ref, v_ref, p_ref, resid_ref, pre_ref,
    gin_ref, dqkv_ref, dres_ref, dpre_ref, up_ref, sums_ref, dsum_ref, x32, up32,
):
    section = lax.axis_index("section")
    amount = SHIFT * section
    count, width = x_ref.shape
    tokens = x32.shape[0]
    heads = dsum_ref.shape[0]
    head_dim = width // heads
    sums_ref[...] = jnp.zeros_like(sums_ref)
    x32[...] = jnp.zeros_like(x32)
    x32[:count, :] = x_ref[...].astype(jnp.float32)
    up32[...] = jnp.zeros_like(up32)
    up32[:count, :] = grad_ref[...].astype(jnp.float32) * live_ref[0, 0]
    to_windows, to_grid = movers(tokens, amount)

    def total(row, values):
        sums_ref[row : row + 1, :] = jnp.sum(values, axis=0, keepdims=True)

    upstream = up32[...]
    total(7, upstream)
    up_ref[...] = upstream.astype(LOW)
    grad_n2 = jnp.zeros((tokens, width), jnp.float32)
    for index in range(wup.shape[1] // width):
        cols = slice(index * width, (index + 1) * width)
        grad_pre = dot_last(up_ref[...], wdown[cols, :]) * gelu_slope(pre_ref[:, cols])
        total(8 + index, grad_pre)
        low = grad_pre.astype(LOW)
        dpre_ref[:, cols] = low
        grad_n2 = grad_n2 + dot_last(low, wup[:, cols])
    _, unit, inv = norm_forward(resid_ref[...], 1.0, 0.0)
    total(5, grad_n2 * unit)
    total(6, grad_n2)
    grad_resid = up32[...] + norm_backward(grad_n2 * gain2[...], unit, inv)
    total(4, grad_resid)
    up32[...] = grad_resid
    dres_ref[...] = grad_resid.astype(LOW)
    grad_att = move(to_windows, dot_last(dres_ref[...], wproj[...]).astype(LOW))
    lanes = head_lanes(head_dim, LOW)
    per = len(lanes)
    for block in range(width // 128):
        cols = slice(block * 128, (block + 1) * 128)
        pieces = ([], [], [])
        bias_sums = [None] * per
        for pair in range(2):
            rows = slice(pair * 2 * PADDED, (pair + 1) * 2 * PADDED)
            q, k, v, ga = q_ref[rows, cols], k_ref[rows, cols], v_ref[rows, cols], grad_att[rows, cols]
            probs, slopes, q_own, k_own, ga_own = [], [], [], [], []
            for h in range(per):
                full = p_ref[pair * heads + block * per + h]
                ga_own.append(ga * lanes[h])
                q_own.append(q * lanes[h])
                k_own.append(k * lanes[h])
                grad_probs = dot_last(ga_own[h], v)
                delta = jnp.sum(full * grad_probs, axis=-1, keepdims=True)
                grad_scores = full * (grad_probs - delta)
                bias_sums[h] = grad_scores if pair == 0 else bias_sums[h] + grad_scores
                slopes.append(grad_scores.astype(LOW))
                probs.append(full.astype(LOW))
            dq = dot_rows(jnp.concatenate(slopes, axis=1), jnp.concatenate(k_own, axis=0))
            dk = dot_first(jnp.concatenate(slopes, axis=0), jnp.concatenate(q_own, axis=0))
            dv = dot_first(jnp.concatenate(probs, axis=0), jnp.concatenate(ga_own, axis=0))
            pieces[0].append(dq * head_dim ** (-0.5))
            pieces[1].append(dk)
            pieces[2].append(dv)
        for h in range(per):
            dsum_ref[block * per + h] = bias_sums[h]
        for index in range(3):
            whole = jnp.concatenate(pieces[index], axis=0)
            if index != 1:
                row = 2 + index // 2
                sums_ref[row : row + 1, cols] = jnp.sum(whole, axis=0, keepdims=True)
            start = index * width + block * 128
            dqkv_ref[:, start : start + 128] = move(to_grid, whole.astype(LOW))
    grad_n1 = dot_last(dqkv_ref[...], wqkv[...])
    _, unit, inv = norm_forward(x32[...], 1.0, 0.0)
    total(0, grad_n1 * unit)
    total(1, grad_n1)
    grad_in = up32[...] + norm_backward(grad_n1 * gain1[...], unit, inv)
    gin_ref[...] = grad_in[:count].astype(LOW)


def weights_kernel(n1, dqkv, att, dres, n2, dpre, hid, up, out_ref):
    _, groups, rows, width = out_ref.shape
    chunk = 0
    for former, latter in ((n1, dqkv), (att, dres), (n2, dpre)):
        for start in range(0, latter.shape[1], width):
            grad = dot_first(former[...], latter[:, start : start + width]).astype(LOW)
            for s in range(groups):
                out_ref[chunk, s] = grad[s * rows : (s + 1) * rows]
            chunk += 1
    tall = hid.shape[1] // groups
    for s in range(groups):
        grad = dot_first(hid[:, s * tall : (s + 1) * tall], up[...]).astype(LOW)
        for j in range(tall // rows):
            out_ref[chunk + j, s] = grad[j * rows : (j + 1) * rows]


def on_chip(kernel, name, outs, scratch, args):
    spec = pl.BlockSpec(memory_space=pltpu.VMEM)
    shapes = [jax.ShapeDtypeStruct(shape, dtype) for shape, dtype in outs]
    return pl.pallas_call(
        kernel,
        out_shape=shapes,
        in_specs=[spec] * len(args),
        out_specs=[spec] * len(shapes),
        scratch_shapes=[pltpu.VMEM(shape, dtype) for shape, dtype in scratch],
        compiler_params=pltpu.CompilerParams(vmem_limit_bytes=60 * 1024 * 1024),
        name=name,
    )(*args)


def bias_onehot():
    places = jnp.arange(PADDED, dtype=jnp.int32)
    rowpos = places // WIN
    colpos = places % WIN
    held = places < WIN * WIN
    offsets = (rowpos[:, None] - rowpos[None, :] + WIN - 1) * (2 * WIN - 1) + (
        colpos[:, None] - colpos[None, :] + WIN - 1
    )
    offsets = jnp.where(held[:, None] & held[None, :], offsets, -1).reshape(-1)
    return (jnp.arange(TABLE, dtype=jnp.int32)[:, None] == offsets[None, :]).astype(jnp.float32)


def local(
    block_input,
    occupied,
    cotangent,
    norm1_gain,
    norm1_bias,
    qkv_weight,
    q_bias,
    v_bias,
    rel_table,
    proj_weight,
    proj_bias,
    norm2_gain,
    norm2_bias,
    fc1_weight,
    fc1_bias,
    fc2_weight,
    fc2_bias,
):
    groups = lax.axis_size("group")
    replicas = lax.axis_size("replica")
    first_section = lax.axis_index("section") == 0
    count, width = block_input.shape[2:]
    hidden = fc1_weight.shape[2]
    heads = rel_table.shape[2]
    tokens = up_to(count, 16)
    slots = (SIDE // WIN) ** 2 * PADDED
    assert block_input.shape[:2] == (1, 1)
    own = block_input[0, 0]
    live = occupied.astype(jnp.float32)
    onehot = bias_onehot()
    bias = jnp.dot(rel_table[0].T, onehot, precision=lax.Precision.HIGHEST)
    bias = jnp.tile(bias.reshape(heads, PADDED, PADDED), (1, 2, 2))
    wqkv, wproj, wup, wdown = gather_all(
        (qkv_weight[0], proj_weight[0], fc1_weight[0], fc2_weight[0]), groups
    )
    high = jnp.float32
    saved_shapes = [
        ((count, width), LOW),
        ((slots, width), LOW),
        ((slots, width), LOW),
        ((slots, width), LOW),
        ((2 * heads, 2 * PADDED, 2 * PADDED), high),
        ((tokens, width), LOW),
        ((tokens, width), high),
        ((tokens, hidden), high),
        ((tokens, width), LOW),
        ((tokens, width), LOW),
        ((tokens, hidden), LOW),
    ]

    def forward(layer_in):
        return on_chip(
            forward_kernel,
            "layer_forward",
            saved_shapes,
            [((tokens, width), high)],
            (
                layer_in, live, norm1_gain, norm1_bias, wqkv, q_bias, v_bias, bias, wproj, proj_bias,
                norm2_gain, norm2_bias, wup, fc1_bias, wdown, fc2_bias,
            ),
        )

    def backward(layer_in, grad, saved):
        _, q, k, v, probs, _, resid, pre, _, _, _ = saved
        return on_chip(
            backward_kernel,
            "layer_backward",
            [
                ((count, width), LOW),
                ((tokens, 3 * width), LOW),
                ((tokens, width), LOW),
                ((tokens, hidden), LOW),
                ((tokens, width), LOW),
                ((up_to(8 + hidden // width, 8), width), high),
                ((heads, 2 * PADDED, 2 * PADDED), high),
            ],
            [((tokens, width), high), ((tokens, width), high)],
            (layer_in, grad, live, norm1_gain, wqkv, wproj, norm2_gain, wup, wdown, q, k, v, probs, resid, pre),
        )

    received = passed_along(forward(own)[0], "section", 1)
    layer_in = jnp.where(first_section, own, received)
    saved = forward(layer_in)
    last_grad = cotangent[0, 0]
    received = passed_along(backward(layer_in, last_grad, saved)[0], "section", -1)
    grad_out = jnp.where(first_section, received, last_grad)
    grad_in, dqkv, dres, dpre, up_low, sums, dsum = backward(layer_in, grad_out, saved)
    _, _, _, _, _, attended, _, _, normed_one, normed_two, hid = saved
    rows = width // groups
    chunks = 4 + 2 * hidden // width
    packed = on_chip(
        weights_kernel,
        "weight_grads",
        [((chunks, groups, rows, width), LOW)],
        [],
        (normed_one, dqkv, attended, dres, normed_two, dpre, hid, up_low),
    )[0]
    blocks = dsum[:, :PADDED, :PADDED] + dsum[:, PADDED:, PADDED:]
    grad_table = lax.dot_general(
        onehot,
        blocks.reshape(heads, -1),
        (((1,), (1,)), ((), ())),
        precision=lax.Precision.HIGHEST,
        preferred_element_type=jnp.float32,
    )
    small = jnp.concatenate([sums, pack_small([grad_table], width)])
    reduced, small_sum = reduce_all(packed, small, groups, replicas)
    ups = hidden // width
    grad_table = unpack_small(small_sum[sums.shape[0] :], [grad_table])[0]

    def widen(piece):
        return piece.transpose(1, 0, 2).reshape(1, rows, -1)

    def one(row):
        return small_sum[row : row + 1]

    return (
        saved[0][None, None, None],
        grad_in[None, None, None],
        one(0),
        one(1),
        widen(reduced[:3]),
        one(2),
        one(3),
        grad_table[None],
        reduced[3][None],
        one(4),
        one(5),
        one(6),
        widen(reduced[4 : 4 + ups]),
        small_sum[8 : 8 + ups].reshape(1, -1),
        reduced[4 + ups :].reshape(1, -1, width),
        one(7),
    )


def solution(mesh):
    in_specs = (
        P(None, ("group", "replica"), None, None),
        P(None, ("group", "replica")),
        P(None, ("group", "replica"), None, None),
        P("section", None),
        P("section", None),
        P("section", "group", None),
        P("section", None),
        P("section", None),
        P("section", None, None),
        P("section", "group", None),
        P("section", None),
        P("section", None),
        P("section", None),
        P("section", "group", None),
        P("section", None),
        P("section", "group", None),
        P("section", None),
    )
    out_specs = (
        P("section", None, ("group", "replica"), None, None),
        P("section", None, ("group", "replica"), None, None),
        P("section", None),
        P("section", None),
        P("section", "group", None),
        P("section", None),
        P("section", None),
        P("section", None, None),
        P("section", "group", None),
        P("section", None),
        P("section", None),
        P("section", None),
        P("section", "group", None),
        P("section", None),
        P("section", "group", None),
        P("section", None),
    )
    return jax.shard_map(local, mesh=mesh, in_specs=in_specs, out_specs=out_specs, check_vma=False)
```

```python
import functools

import jax
import jax.numpy as jnp
from jax import lax
from jax.experimental import pallas as pl
from jax.experimental.pallas import tpu as pltpu
from jax.sharding import PartitionSpec as P

WIN = 7
SHIFT = 3
SIDE = 14
TABLE = 169


norm_eps = 1e-05
mask_fill = -100.0
root_half = 0.7071067811865476
inv_root_two_pi = 0.3989422804014327

MESH = pl.DeviceIdType.MESH
LAG = 3


def rounds_of(devices):
    count = devices.bit_length() - 1
    assert devices == 1 << count, "power"
    return count


def chain_place(rank, devices):
    half = devices // 2
    left = rank < half
    is_mid = (rank == half - 1) | (rank == half)
    has_outer = (left & (rank > 0)) | (~left & (rank < devices - 1))
    inner = jnp.where(left, rank + 1, rank - 1)
    outer = jnp.where(left, jnp.maximum(rank - 1, 0), jnp.minimum(rank + 1, devices - 1))
    return is_mid, has_outer, inner, outer


def reduce_kernel(
    groups,
    replicas,
    grads,
    small,
    qkv_out,
    proj_out,
    up_out,
    down_out,
    small_out,
    *scratch,
):
    rounds = rounds_of(groups)
    recv_bufs = scratch[:rounds]
    acc_bufs = scratch[rounds : 2 * rounds]
    (
        chain_buf,
        total_buf,
        small_send,
        small_recv,
        send_sem,
        recv_sem,
        chain_send,
        chain_recv,
        back_send,
        back_recv,
        small_ssem,
        small_rsem,
    ) = scratch[2 * rounds :]
    chunks = grads.shape[0]
    me = lax.axis_index("group")
    rank = lax.axis_index("replica")
    is_mid, has_outer, inner, outer = chain_place(rank, replicas)
    bits = [lax.rem(me // (1 << r), 2) for r in range(rounds)]
    partners = [me + (1 - 2 * bits[r]) * (1 << r) for r in range(rounds)]

    barrier = pltpu.get_barrier_semaphore()
    for partner in partners:
        pl.semaphore_signal(barrier, inc=1, device_id={"group": partner}, device_id_type=MESH)
    pl.semaphore_signal(barrier, inc=1, device_id={"replica": inner}, device_id_type=MESH)

    @pl.when(has_outer)
    def _():
        pl.semaphore_signal(barrier, inc=1, device_id={"replica": outer}, device_id_type=MESH)

    pl.semaphore_wait(barrier, rounds + 1 + has_outer.astype(jnp.int32))

    def round_copy(r, j, u):
        source = grads if r == 0 else acc_bufs[r - 1]
        return pltpu.make_async_remote_copy(
            src_ref=source.at[j, 2 * u + 1 - bits[r]],
            dst_ref=recv_bufs[r].at[j, u],
            send_sem=send_sem.at[r, j, u],
            recv_sem=recv_sem.at[r, j, u],
            device_id={"group": partners[r]},
            device_id_type=MESH,
        )

    mid_slot = is_mid.astype(jnp.int32)

    def chain_copy(j, slot):
        return pltpu.make_async_remote_copy(
            src_ref=acc_bufs[rounds - 1].at[j, 0],
            dst_ref=chain_buf.at[slot, j],
            send_sem=chain_send.at[j],
            recv_sem=chain_recv.at[slot, j],
            device_id={"replica": inner},
            device_id_type=MESH,
        )

    def back_copy(j):
        return pltpu.make_async_remote_copy(
            src_ref=total_buf.at[j],
            dst_ref=total_buf.at[j],
            send_sem=back_send.at[j],
            recv_sem=back_recv.at[j],
            device_id={"replica": outer},
            device_id_type=MESH,
        )

    def small_copy(k, slot, target):
        return pltpu.make_async_remote_copy(
            src_ref=small_send.at[k],
            dst_ref=small_recv.at[slot],
            send_sem=small_ssem.at[k],
            recv_sem=small_rsem.at[slot],
            device_id=target,
            device_id_type=MESH,
        )

    def add_up(former, latter):
        return (former.astype(jnp.float32) + latter.astype(jnp.float32)).astype(jnp.bfloat16)

    def fold_round(r, j):
        for u in range(groups >> (r + 1)):
            round_copy(r, j, u).wait_recv()
            source = grads if r == 0 else acc_bufs[r - 1]
            acc_bufs[r][j, u] = add_up(source[j, 2 * u + bits[r]], recv_bufs[r][j, u])
        if r + 1 < rounds:
            for u in range(groups >> (r + 2)):
                round_copy(r + 1, j, u).start()
        else:

            @pl.when(~has_outer)
            def _():
                chain_copy(j, mid_slot).start()

    last = acc_bufs[rounds - 1]

    def from_outer(j):
        @pl.when(has_outer)
        def _():
            chain_copy(j, 0).wait_recv()
            last[j, 0] = add_up(last[j, 0], chain_buf[0, j])
            chain_copy(j, mid_slot).start()

    def meet(j):
        @pl.when(is_mid)
        def _():
            chain_copy(j, 1).wait_recv()
            total_buf[j] = add_up(last[j, 0], chain_buf[1, j])

        @pl.when(~is_mid)
        def _():
            back_copy(j).wait_recv()

        @pl.when(has_outer)
        def _():
            back_copy(j).start()

        rows, width = total_buf.shape[1:]
        value = total_buf[j].astype(jnp.float32)
        first = 0
        for out in (qkv_out, proj_out, up_out, down_out):
            tall = out is down_out
            parts = out.shape[0] // rows if tall else out.shape[1] // width

            @pl.when((j >= first) & (j < first + parts))
            def _(out=out, tall=tall, first=first):
                if tall:
                    out[pl.ds(pl.multiple_of((j - first) * rows, rows), rows), :] = value
                else:
                    out[:, pl.ds(pl.multiple_of((j - first) * width, width), width)] = value

            first += parts

    small_send[0] = small[...]
    if rounds > 0:
        small_copy(0, 0, {"group": partners[0]}).start()

    @pl.loop(0, chunks)
    def _(j):
        for u in range(groups // 2):
            round_copy(0, j, u).start()

    def small_step(k):
        if k < rounds:
            small_copy(k, k, {"group": partners[k]}).wait_recv()
            small_send[k + 1] = small_send[k] + small_recv[k]
            if k + 1 < rounds:
                small_copy(k + 1, k + 1, {"group": partners[k + 1]}).start()
            else:

                @pl.when(~has_outer)
                def _():
                    small_copy(rounds, rounds + mid_slot, {"replica": inner}).start()
        elif k == rounds:

            @pl.when(has_outer)
            def _():
                small_copy(rounds, rounds, {"replica": inner}).wait_recv()
                small_send[rounds] = small_send[rounds] + small_recv[rounds]
                small_copy(rounds, rounds + mid_slot, {"replica": inner}).start()
        else:

            @pl.when(is_mid)
            def _():
                small_copy(rounds, rounds + 1, {"replica": inner}).wait_recv()
                small_send[rounds + 1] = small_send[rounds] + small_recv[rounds + 1]

            @pl.when(~is_mid)
            def _():
                small_copy(rounds + 1, rounds + 2, {"replica": outer}).wait_recv()
                small_send[rounds + 1] = small_recv[rounds + 2]

            @pl.when(has_outer)
            def _():
                small_copy(rounds + 1, rounds + 2, {"replica": outer}).start()

            small_out[...] = small_send[rounds + 1]

    stages = [functools.partial(fold_round, r) for r in range(rounds)] + [from_outer, meet]

    @pl.loop(0, chunks + LAG * (len(stages) - 1))
    def _(step):
        for depth, stage in enumerate(stages):
            j = step - LAG * depth

            @pl.when((j >= 0) & (j < chunks))
            def _():
                stage(j)

            @pl.when(step == LAG * depth)
            def _():
                small_step(depth)

    @pl.loop(0, chunks)
    def _(j):
        for r in range(rounds):
            for u in range(groups >> (r + 1)):
                round_copy(r, j, u).wait_send()
        chain_copy(j, mid_slot).wait_send()

        @pl.when(has_outer)
        def _():
            back_copy(j).wait_send()

    for k in range(rounds):
        small_copy(k, k, {"group": partners[k]}).wait_send()
    small_copy(rounds, rounds + mid_slot, {"replica": inner}).wait_send()

    @pl.when(has_outer)
    def _():
        small_copy(rounds + 1, rounds + 2, {"replica": outer}).wait_send()


def reduce_all(grads, small, shapes, groups, replicas):
    chunks, _, rows, cols = grads.shape
    rounds = rounds_of(groups)
    low = jnp.bfloat16
    halves = [groups >> (r + 1) for r in range(rounds)]
    scratch = (
        [pltpu.VMEM((chunks, half, rows, cols), low) for half in halves]
        + [pltpu.VMEM((chunks, half, rows, cols), low) for half in halves]
        + [
            pltpu.VMEM((2, chunks, rows, cols), low),
            pltpu.VMEM((chunks, rows, cols), low),
            pltpu.VMEM((rounds + 2,) + small.shape, jnp.float32),
            pltpu.VMEM((rounds + 3,) + small.shape, jnp.float32),
            pltpu.SemaphoreType.DMA((rounds, chunks, groups // 2)),
            pltpu.SemaphoreType.DMA((rounds, chunks, groups // 2)),
            pltpu.SemaphoreType.DMA((chunks,)),
            pltpu.SemaphoreType.DMA((2, chunks)),
            pltpu.SemaphoreType.DMA((chunks,)),
            pltpu.SemaphoreType.DMA((chunks,)),
            pltpu.SemaphoreType.DMA((rounds + 2,)),
            pltpu.SemaphoreType.DMA((rounds + 3,)),
        ]
    )
    return pl.pallas_call(
        functools.partial(reduce_kernel, groups, replicas),
        out_shape=(
            *[jax.ShapeDtypeStruct(shape, jnp.float32) for shape in shapes],
            jax.ShapeDtypeStruct(small.shape, jnp.float32),
        ),
        in_specs=[pl.BlockSpec(memory_space=pltpu.VMEM)] * 2,
        out_specs=[pl.BlockSpec(memory_space=pltpu.VMEM)] * 5,
        scratch_shapes=scratch,
        compiler_params=pltpu.CompilerParams(
            collective_id=1, has_side_effects=True, vmem_limit_bytes=60 * 1024 * 1024
        ),
        name="grad_reduce",
    )(grads, small)


def gather_kernel(groups, *refs):
    count = (len(refs) - 7) // 2
    parts = refs[:count]
    wholes = refs[count : 2 * count]
    own_sem, x_send, x_recv, z_send, z_recv, core_send, core_recv = refs[2 * count :]
    steps = rounds_of(groups) - 1
    me = lax.axis_index("group")
    rank = lax.axis_index("replica")
    parity = lax.rem(rank, 2)
    mate = rank + 1 - 2 * parity
    flips = [(1 - 2 * lax.rem(me // (1 << r), 2)) * (1 << r) for r in range(steps + 1)]

    barrier = pltpu.get_barrier_semaphore()
    for flip in flips:
        pl.semaphore_signal(barrier, inc=1, device_id={"group": me + flip}, device_id_type=MESH)
    pl.semaphore_signal(barrier, inc=1, device_id={"replica": mate}, device_id_type=MESH)
    pl.semaphore_wait(barrier, steps + 2)

    held = [me]
    for step in range(steps):
        held = held + [device + flips[step + 1] for device in held]

    def half_of(i, k, half, source):
        height = parts[i].shape[0]
        tall = height // 2
        if source and k == 0:
            return parts[i].at[pl.ds(pl.multiple_of(half * tall, tall), tall), :]
        start = pl.multiple_of(held[k] * height + half * tall, tall)
        return wholes[i].at[pl.ds(start, tall), :]

    def half_copy(i, k, half, sems, target):
        return pltpu.make_async_remote_copy(
            src_ref=half_of(i, k, half, True),
            dst_ref=half_of(i, k, half, False),
            send_sem=sems[0],
            recv_sem=sems[1],
            device_id=target,
            device_id_type=MESH,
        )

    def x_copy(i, step, k):
        sems = (x_send.at[i, step, k], x_recv.at[i, step, k])
        return half_copy(i, k, parity, sems, {"group": me + flips[step + 1]})

    def z_copy(i, k):
        return half_copy(i, k, parity, (z_send.at[i, k], z_recv.at[i, k]), {"replica": mate})

    def core_copy(i, k, which):
        half = parity if which == 0 else 1 - parity
        sems = (core_send.at[i, k, which], core_recv.at[i, k, which])
        return half_copy(i, k, half, sems, {"group": me + flips[0]})

    def own_copy(i):
        height = parts[i].shape[0]
        rows = pl.ds(pl.multiple_of(me * height, height), height)
        return pltpu.make_async_copy(parts[i], wholes[i].at[rows, :], own_sem.at[i])

    for i in range(count):
        for step in range(steps):
            x_copy(i, step, 0).start()
    for i in range(count):
        core_copy(i, 0, 0).start()
        core_copy(i, 0, 1).start()
        own_copy(i).start()
    for i in range(count + 1):
        if i < count:
            for step in range(steps):
                for k in range(1 << step):
                    x_copy(i, step, k).wait_recv()
                    index = k + (1 << step)
                    for later in range(step + 1, steps):
                        x_copy(i, later, index).start()
                    z_copy(i, index).start()
                    core_copy(i, index, 0).start()
        if i > 0:
            for k in range(1, len(held)):
                z_copy(i - 1, k).wait_recv()
                core_copy(i - 1, k, 1).start()
    for i in range(count):
        own_copy(i).wait()
        for k in range(len(held)):
            for which in range(2):
                core_copy(i, k, which).wait_recv()
                core_copy(i, k, which).wait_send()
            if k > 0:
                z_copy(i, k).wait_send()
        for step in range(steps):
            for k in range(1 << step):
                x_copy(i, step, k).wait_send()


def gather_all(parts, groups, replicas):
    count = len(parts)
    rounds = rounds_of(groups)
    assert rounds > 1 and replicas % 2 == 0
    half = groups // 2
    dma = pltpu.SemaphoreType.DMA
    return pl.pallas_call(
        functools.partial(gather_kernel, groups),
        out_shape=[
            jax.ShapeDtypeStruct((groups * part.shape[0], part.shape[1]), part.dtype)
            for part in parts
        ],
        in_specs=[pl.BlockSpec(memory_space=pltpu.VMEM)] * count,
        out_specs=[pl.BlockSpec(memory_space=pltpu.VMEM)] * count,
        scratch_shapes=[
            dma((count,)),
            dma((count, rounds - 1, half)),
            dma((count, rounds - 1, half)),
            dma((count, half)),
            dma((count, half)),
            dma((count, half, 2)),
            dma((count, half, 2)),
        ],
        compiler_params=pltpu.CompilerParams(collective_id=2, has_side_effects=True),
        name="weight_gather",
    )(*parts)


def pack_small(terms, width):
    flat = jnp.concatenate([term.reshape(-1) for term in terms])
    rows = -(-flat.shape[0] // width)
    rows = -(-rows // 8) * 8
    return jnp.pad(flat, (0, rows * width - flat.shape[0])).reshape(rows, width)


def unpack_small(packed, terms):
    flat = packed.reshape(-1)
    found = []
    start = 0
    for term in terms:
        found.append(flat[start : start + term.size].reshape(term.shape))
        start += term.size
    return found


def passed_along(shard, axis, by):
    devices = lax.axis_size(axis)
    pairs = [(i, i + by) for i in range(devices) if 0 <= i + by < devices]
    return lax.ppermute(shard, axis, pairs)


def norm_forward(values, gain_vec, bias_vec):
    centered = values - jnp.mean(values, axis=-1, keepdims=True)
    scale_inv = lax.rsqrt(jnp.mean(centered * centered, axis=-1, keepdims=True) + norm_eps)
    normed = centered * scale_inv
    return (normed * gain_vec + bias_vec, normed, scale_inv)


def norm_backward(grad_normed, normed, scale_inv):
    first_mean = jnp.mean(grad_normed, axis=-1, keepdims=True)
    second_mean = jnp.mean(grad_normed * normed, axis=-1, keepdims=True)
    return scale_inv * (grad_normed - first_mean - normed * second_mean)


def gelu_value(pre_act):
    return 0.5 * pre_act * (1.0 + lax.erf(pre_act * root_half))


def gelu_slope(pre_act):
    return (
        0.5 * (1.0 + lax.erf(pre_act * root_half))
        + pre_act * jnp.exp(-0.5 * pre_act * pre_act) * inv_root_two_pi
    )


NEG = -1e30
LOW = jnp.bfloat16
PADDED = 64


def up_to(count, step):
    return -(-count // step) * step


def div_win(values):
    return jnp.right_shift(values * 37, 8)


def dot_rows(former, latter):
    return lax.dot_general(former, latter, (((1,), (0,)), ((), ())), preferred_element_type=jnp.float32)


def dot_last(former, latter):
    return lax.dot_general(former, latter, (((1,), (1,)), ((), ())), preferred_element_type=jnp.float32)


def dot_first(former, latter):
    return lax.dot_general(former, latter, (((0,), (0,)), ((), ())), preferred_element_type=jnp.float32)


def place_of(slot, amount):
    window = jnp.right_shift(slot, 6)
    inside = jnp.bitwise_and(slot, PADDED - 1)
    in_row = div_win(inside)
    row = jnp.right_shift(window, 1) * WIN + in_row
    col = jnp.bitwise_and(window, 1) * WIN + inside - in_row * WIN
    held = inside < WIN * WIN
    old_row = row + amount
    old_row = jnp.where(old_row >= SIDE, old_row - SIDE, old_row)
    old_col = col + amount
    old_col = jnp.where(old_col >= SIDE, old_col - SIDE, old_col)
    token = jnp.where(held, old_row * SIDE + old_col, -1)
    return window, row, col, token, held


def movers(tokens, amount):
    slots = (SIDE // WIN) ** 2 * PADDED
    down = lax.broadcasted_iota(jnp.int32, (slots, tokens), 0)
    across = lax.broadcasted_iota(jnp.int32, (slots, tokens), 1)
    to_windows = (place_of(down, amount)[3] == across).astype(jnp.float32).astype(LOW)
    down = lax.broadcasted_iota(jnp.int32, (tokens, slots), 0)
    across = lax.broadcasted_iota(jnp.int32, (tokens, slots), 1)
    to_grid = (place_of(across, amount)[3] == down).astype(jnp.float32).astype(LOW)
    return to_windows, to_grid


def move(mover, values):
    return dot_rows(mover, values).astype(LOW)


def pair_mask(pair, amount, factor):
    def parts(axis):
        slot = lax.broadcasted_iota(jnp.int32, (2 * PADDED, 2 * PADDED), axis) + pair * 2 * PADDED
        window, row, col, _, held = place_of(slot, amount)
        bands = []
        for line in (row, col):
            bands.append(
                (line >= SIDE - WIN).astype(jnp.int32) + (line >= SIDE - SHIFT).astype(jnp.int32)
            )
        return window, 3 * bands[0] + bands[1], held

    window_q, label_q, _ = parts(0)
    window_k, label_k, held_k = parts(1)
    mask = jnp.where(label_q != label_k, mask_fill * factor, 0.0)
    return jnp.where((window_q == window_k) & held_k, mask, NEG)


def head_lanes(head_dim, dtype):
    lane = lax.broadcasted_iota(jnp.int32, (2 * PADDED, 128), 1)
    return [
        ((lane >= h * head_dim) & (lane < (h + 1) * head_dim)).astype(jnp.float32).astype(dtype)
        for h in range(128 // head_dim)
    ]


def forward_kernel(
    x_ref, live_ref, gain1, bias1, wqkv, qb, vb, bias_ref, wproj, projb, gain2, bias2, wup, upb, wdown, downb,
    act_ref, q_ref, k_ref, v_ref, p_ref, att_ref, resid_ref, pre_ref, n1_ref, n2_ref, hid_ref, x32,
):
    section = lax.axis_index("section")
    amount = SHIFT * section
    factor = section.astype(jnp.float32)
    count, width = x_ref.shape
    tokens = x32.shape[0]
    heads = bias_ref.shape[0]
    head_dim = width // heads
    x32[...] = jnp.zeros_like(x32)
    x32[:count, :] = x_ref[...].astype(jnp.float32)
    to_windows, to_grid = movers(tokens, amount)
    normed, _, _ = norm_forward(x32[...], gain1[...], bias1[...])
    n1_ref[...] = normed.astype(LOW)
    query = dot_rows(n1_ref[...], wqkv[:, :width]) + qb[...]
    q_ref[...] = move(to_windows, (query * head_dim ** (-0.5)).astype(LOW))
    k_ref[...] = move(to_windows, dot_rows(n1_ref[...], wqkv[:, width : 2 * width]).astype(LOW))
    v_ref[...] = move(to_windows, (dot_rows(n1_ref[...], wqkv[:, 2 * width :]) + vb[...]).astype(LOW))
    lanes = head_lanes(head_dim, LOW)
    per = len(lanes)
    columns = []
    for pair in range(2):
        mask = pair_mask(pair, amount, factor)
        rows = slice(pair * 2 * PADDED, (pair + 1) * 2 * PADDED)
        found = []
        for block in range(width // 128):
            cols = slice(block * 128, (block + 1) * 128)
            q, k, v = q_ref[rows, cols], k_ref[rows, cols], v_ref[rows, cols]
            probs = []
            values = []
            for h in range(per):
                scores = dot_last(q * lanes[h], k) + bias_ref[block * per + h] + mask
                raised = jnp.exp(scores - jnp.max(scores, axis=-1, keepdims=True))
                full = raised / jnp.sum(raised, axis=-1, keepdims=True)
                p_ref[pair * heads + block * per + h] = full
                probs.append(full.astype(LOW))
                values.append(v * lanes[h])
            found.append(
                dot_rows(jnp.concatenate(probs, axis=1), jnp.concatenate(values, axis=0)).astype(LOW)
            )
        columns.append(jnp.concatenate(found, axis=1))
    attended = move(to_grid, jnp.concatenate(columns, axis=0))
    att_ref[...] = attended
    resid = x32[...] + (dot_rows(attended, wproj[...]) + projb[...])
    resid_ref[...] = resid
    normed, _, _ = norm_forward(resid, gain2[...], bias2[...])
    n2_ref[...] = normed.astype(LOW)
    for start in range(0, wup.shape[1], width):
        cols = slice(start, start + width)
        pre = dot_rows(n2_ref[...], wup[:, cols]) + upb[:, cols]
        pre_ref[:, cols] = pre
        hid_ref[:, cols] = gelu_value(pre).astype(LOW)
    result = resid_ref[...] + (dot_rows(hid_ref[...], wdown[...]) + downb[...])
    act_ref[...] = (result * live_ref[0, 0])[:count].astype(LOW)


def backward_kernel(
    x_ref, grad_ref, live_ref, gain1, wqkv, wproj, gain2, wup, wdown,
    q_ref, k_ref, v_ref, p_ref, resid_ref, pre_ref,
    gin_ref, dqkv_ref, dres_ref, dpre_ref, up_ref, sums_ref, dsum_ref, x32, up32,
):
    section = lax.axis_index("section")
    amount = SHIFT * section
    count, width = x_ref.shape
    tokens = x32.shape[0]
    heads = dsum_ref.shape[0]
    head_dim = width // heads
    sums_ref[...] = jnp.zeros_like(sums_ref)
    x32[...] = jnp.zeros_like(x32)
    x32[:count, :] = x_ref[...].astype(jnp.float32)
    up32[...] = jnp.zeros_like(up32)
    up32[:count, :] = grad_ref[...].astype(jnp.float32) * live_ref[0, 0]
    to_windows, to_grid = movers(tokens, amount)

    def total(row, values):
        sums_ref[row : row + 1, :] = jnp.sum(values, axis=0, keepdims=True)

    upstream = up32[...]
    total(7, upstream)
    up_ref[...] = upstream.astype(LOW)
    grad_n2 = jnp.zeros((tokens, width), jnp.float32)
    for index in range(wup.shape[1] // width):
        cols = slice(index * width, (index + 1) * width)
        grad_pre = dot_last(up_ref[...], wdown[cols, :]) * gelu_slope(pre_ref[:, cols])
        total(8 + index, grad_pre)
        low = grad_pre.astype(LOW)
        dpre_ref[:, cols] = low
        grad_n2 = grad_n2 + dot_last(low, wup[:, cols])
    _, unit, inv = norm_forward(resid_ref[...], 1.0, 0.0)
    total(5, grad_n2 * unit)
    total(6, grad_n2)
    grad_resid = up32[...] + norm_backward(grad_n2 * gain2[...], unit, inv)
    total(4, grad_resid)
    up32[...] = grad_resid
    dres_ref[...] = grad_resid.astype(LOW)
    grad_att = move(to_windows, dot_last(dres_ref[...], wproj[...]).astype(LOW))
    lanes = head_lanes(head_dim, LOW)
    per = len(lanes)
    for block in range(width // 128):
        cols = slice(block * 128, (block + 1) * 128)
        pieces = ([], [], [])
        bias_sums = [None] * per
        for pair in range(2):
            rows = slice(pair * 2 * PADDED, (pair + 1) * 2 * PADDED)
            q, k, v, ga = q_ref[rows, cols], k_ref[rows, cols], v_ref[rows, cols], grad_att[rows, cols]
            probs, slopes, q_own, k_own, ga_own = [], [], [], [], []
            for h in range(per):
                full = p_ref[pair * heads + block * per + h]
                ga_own.append(ga * lanes[h])
                q_own.append(q * lanes[h])
                k_own.append(k * lanes[h])
                grad_probs = dot_last(ga_own[h], v)
                delta = jnp.sum(full * grad_probs, axis=-1, keepdims=True)
                grad_scores = full * (grad_probs - delta)
                bias_sums[h] = grad_scores if pair == 0 else bias_sums[h] + grad_scores
                slopes.append(grad_scores.astype(LOW))
                probs.append(full.astype(LOW))
            dq = dot_rows(jnp.concatenate(slopes, axis=1), jnp.concatenate(k_own, axis=0))
            dk = dot_first(jnp.concatenate(slopes, axis=0), jnp.concatenate(q_own, axis=0))
            dv = dot_first(jnp.concatenate(probs, axis=0), jnp.concatenate(ga_own, axis=0))
            pieces[0].append(dq * head_dim ** (-0.5))
            pieces[1].append(dk)
            pieces[2].append(dv)
        for h in range(per):
            dsum_ref[block * per + h] = bias_sums[h]
        for index in range(3):
            whole = jnp.concatenate(pieces[index], axis=0)
            if index != 1:
                row = 2 + index // 2
                sums_ref[row : row + 1, cols] = jnp.sum(whole, axis=0, keepdims=True)
            start = index * width + block * 128
            dqkv_ref[:, start : start + 128] = move(to_grid, whole.astype(LOW))
    grad_n1 = dot_last(dqkv_ref[...], wqkv[...])
    _, unit, inv = norm_forward(x32[...], 1.0, 0.0)
    total(0, grad_n1 * unit)
    total(1, grad_n1)
    grad_in = up32[...] + norm_backward(grad_n1 * gain1[...], unit, inv)
    gin_ref[...] = grad_in[:count].astype(LOW)


def weights_kernel(n1, dqkv, att, dres, n2, dpre, hid, up, out_ref):
    _, groups, rows, width = out_ref.shape
    chunk = 0
    for former, latter in ((n1, dqkv), (att, dres), (n2, dpre)):
        for start in range(0, latter.shape[1], width):
            grad = dot_first(former[...], latter[:, start : start + width]).astype(LOW)
            for s in range(groups):
                out_ref[chunk, s] = grad[s * rows : (s + 1) * rows]
            chunk += 1
    tall = hid.shape[1] // groups
    for s in range(groups):
        grad = dot_first(hid[:, s * tall : (s + 1) * tall], up[...]).astype(LOW)
        for j in range(tall // rows):
            out_ref[chunk + j, s] = grad[j * rows : (j + 1) * rows]


def on_chip(kernel, name, outs, scratch, args):
    spec = pl.BlockSpec(memory_space=pltpu.VMEM)
    shapes = [jax.ShapeDtypeStruct(shape, dtype) for shape, dtype in outs]
    return pl.pallas_call(
        kernel,
        out_shape=shapes,
        in_specs=[spec] * len(args),
        out_specs=[spec] * len(shapes),
        scratch_shapes=[pltpu.VMEM(shape, dtype) for shape, dtype in scratch],
        compiler_params=pltpu.CompilerParams(vmem_limit_bytes=60 * 1024 * 1024),
        name=name,
    )(*args)


def bias_onehot():
    places = jnp.arange(PADDED, dtype=jnp.int32)
    rowpos = places // WIN
    colpos = places % WIN
    held = places < WIN * WIN
    offsets = (rowpos[:, None] - rowpos[None, :] + WIN - 1) * (2 * WIN - 1) + (
        colpos[:, None] - colpos[None, :] + WIN - 1
    )
    offsets = jnp.where(held[:, None] & held[None, :], offsets, -1).reshape(-1)
    return (jnp.arange(TABLE, dtype=jnp.int32)[:, None] == offsets[None, :]).astype(jnp.float32)


def local(
    block_input,
    occupied,
    cotangent,
    norm1_gain,
    norm1_bias,
    qkv_weight,
    q_bias,
    v_bias,
    rel_table,
    proj_weight,
    proj_bias,
    norm2_gain,
    norm2_bias,
    fc1_weight,
    fc1_bias,
    fc2_weight,
    fc2_bias,
):
    groups = lax.axis_size("group")
    replicas = lax.axis_size("replica")
    first_section = lax.axis_index("section") == 0
    count, width = block_input.shape[2:]
    hidden = fc1_weight.shape[2]
    heads = rel_table.shape[2]
    tokens = up_to(count, 16)
    slots = (SIDE // WIN) ** 2 * PADDED
    assert block_input.shape[:2] == (1, 1)
    own = block_input[0, 0]
    live = occupied.astype(jnp.float32)
    onehot = bias_onehot()
    bias = jnp.dot(rel_table[0].T, onehot, precision=lax.Precision.HIGHEST)
    bias = jnp.tile(bias.reshape(heads, PADDED, PADDED), (1, 2, 2))
    wqkv, wproj, wup, wdown = gather_all(
        (qkv_weight[0], proj_weight[0], fc1_weight[0], fc2_weight[0]), groups, replicas
    )
    high = jnp.float32
    saved_shapes = [
        ((count, width), LOW),
        ((slots, width), LOW),
        ((slots, width), LOW),
        ((slots, width), LOW),
        ((2 * heads, 2 * PADDED, 2 * PADDED), high),
        ((tokens, width), LOW),
        ((tokens, width), high),
        ((tokens, hidden), high),
        ((tokens, width), LOW),
        ((tokens, width), LOW),
        ((tokens, hidden), LOW),
    ]

    def forward(layer_in):
        return on_chip(
            forward_kernel,
            "layer_forward",
            saved_shapes,
            [((tokens, width), high)],
            (
                layer_in, live, norm1_gain, norm1_bias, wqkv, q_bias, v_bias, bias, wproj, proj_bias,
                norm2_gain, norm2_bias, wup, fc1_bias, wdown, fc2_bias,
            ),
        )

    def backward(layer_in, grad, saved):
        _, q, k, v, probs, _, resid, pre, _, _, _ = saved
        return on_chip(
            backward_kernel,
            "layer_backward",
            [
                ((count, width), LOW),
                ((tokens, 3 * width), LOW),
                ((tokens, width), LOW),
                ((tokens, hidden), LOW),
                ((tokens, width), LOW),
                ((up_to(8 + hidden // width, 8), width), high),
                ((heads, 2 * PADDED, 2 * PADDED), high),
            ],
            [((tokens, width), high), ((tokens, width), high)],
            (layer_in, grad, live, norm1_gain, wqkv, wproj, norm2_gain, wup, wdown, q, k, v, probs, resid, pre),
        )

    received = passed_along(forward(own)[0], "section", 1)
    layer_in = jnp.where(first_section, own, received)
    saved = forward(layer_in)
    last_grad = cotangent[0, 0]
    received = passed_along(backward(layer_in, last_grad, saved)[0], "section", -1)
    grad_out = jnp.where(first_section, received, last_grad)
    grad_in, dqkv, dres, dpre, up_low, sums, dsum = backward(layer_in, grad_out, saved)
    _, _, _, _, _, attended, _, _, normed_one, normed_two, hid = saved
    rows = width // groups
    chunks = 4 + 2 * hidden // width
    packed = on_chip(
        weights_kernel,
        "weight_grads",
        [((chunks, groups, rows, width), LOW)],
        [],
        (normed_one, dqkv, attended, dres, normed_two, dpre, hid, up_low),
    )[0]
    blocks = dsum[:, :PADDED, :PADDED] + dsum[:, PADDED:, PADDED:]
    grad_table = lax.dot_general(
        onehot,
        blocks.reshape(heads, -1),
        (((1,), (1,)), ((), ())),
        precision=lax.Precision.HIGHEST,
        preferred_element_type=jnp.float32,
    )
    small = jnp.concatenate([sums, pack_small([grad_table], width)])
    shapes = [part.shape[1:] for part in (qkv_weight, proj_weight, fc1_weight, fc2_weight)]
    grad_qkv, grad_proj, grad_up, grad_down, small_sum = reduce_all(
        packed, small, shapes, groups, replicas
    )
    ups = hidden // width
    grad_table = unpack_small(small_sum[sums.shape[0] :], [grad_table])[0]

    def one(row):
        return small_sum[row : row + 1]

    return (
        saved[0][None, None, None],
        grad_in[None, None, None],
        one(0),
        one(1),
        grad_qkv[None],
        one(2),
        one(3),
        grad_table[None],
        grad_proj[None],
        one(4),
        one(5),
        one(6),
        grad_up[None],
        small_sum[8 : 8 + ups].reshape(1, -1),
        grad_down[None],
        one(7),
    )


def solution(mesh):
    in_specs = (
        P(None, ("group", "replica"), None, None),
        P(None, ("group", "replica")),
        P(None, ("group", "replica"), None, None),
        P("section", None),
        P("section", None),
        P("section", "group", None),
        P("section", None),
        P("section", None),
        P("section", None, None),
        P("section", "group", None),
        P("section", None),
        P("section", None),
        P("section", None),
        P("section", "group", None),
        P("section", None),
        P("section", "group", None),
        P("section", None),
    )
    out_specs = (
        P("section", None, ("group", "replica"), None, None),
        P("section", None, ("group", "replica"), None, None),
        P("section", None),
        P("section", None),
        P("section", "group", None),
        P("section", None),
        P("section", None),
        P("section", None, None),
        P("section", "group", None),
        P("section", None),
        P("section", None),
        P("section", None),
        P("section", "group", None),
        P("section", None),
        P("section", "group", None),
        P("section", None),
    )
    return jax.shard_map(local, mesh=mesh, in_specs=in_specs, out_specs=out_specs, check_vma=False)
```
